512 devices in a mesh: vocab: 16 (over z_hi, y, core), dp: 8 (over z_lo), replica: 4 (over x).
Axes of the slice: x: 4, y: 4, z: 16 (z_hi: 2, z_lo: 8; z = z_hi * 8 + z_lo), core: 2. Of those that a mesh axis runs over, the one named last changes fastest.
Arguments:
- hidden: bfloat16 [1024, 4096], P('dp'), may hold values from -6 to 6
- head_weight: bfloat16 [4096, 65536], P('dp', ('vocab', 'replica')), may hold values from -0.09375 to 0.09375
- head_bias: float32 [65536], P(('vocab', 'replica')), may hold values from -2.5 to 2.5
- rep_cotangent: float32 [64, 65536], P('dp', ('vocab', 'replica')), may hold values from -6 to 6
- lengths: int32 [64], P('dp'), may hold values from 1 to 16, 640 in all
Outputs:
- pooled: float32 [64, 65536], P('dp', ('vocab', 'replica'))
- term_mean: float32 [65536], P(('vocab', 'replica'))
- bias_grad: float32 [65536], P(('vocab', 'replica'))
- weight_grad: float32 [4096, 65536], P('dp', ('vocab', 'replica'))
- input_grad: float32 [1024, 4096], P(('vocab', 'replica'), 'dp')
The draws below stay inside these ranges and needn't reach their ends.
Inputs may be any that keep to these rules, and one draw needn't show every extreme that they name: `lengths`: each sequence has at least one live token; some sequence has all 16 live.
All inputs are finite; a program needn't handle non-finite values. No bound on the sum of `lengths` on one device may be relied on, other than what follows from the above.
Results may differ from the reference program's by a relative error of at most 0.015.
Values may be sent and summed in bfloat16 or wider, within the bound.
No kernel may reach another device: no remote copies, remote signals or barrier semaphores. Data moves between devices by JAX's collectives and lax.ppermute only.
A program may use at most 64 MiB of HBM per device.

```python
import math
import jax
import jax.numpy as jnp
import numpy as np
from jax import lax

D = 4096
LEN = 16
VOCAB = 65536
SEQS = 64
TOKENS = 1024
N_DP = 8


def levels(rng, shape, cuts, least, top_value):
    def one(dim, shards_of):
        heights = jax.random.uniform(jax.random.fold_in(jax.random.fold_in(rng, 6), dim), (shards_of,), jnp.float32, least / len(cuts), top_value / len(cuts))
        return jnp.repeat(jnp.exp(heights), shape[dim] // shards_of).reshape((-1,) + (1,) * (len(shape) - dim - 1))

    factor_of = one(*cuts[0])
    for cut in cuts[1:]:
        factor_of = factor_of * one(*cut)
    return factor_of


def profile(amount, total, reach, lean):
    portions = [(1 << 20) // math.isqrt(standing ** lean) + 1 for standing in range(2, amount + 1)]
    surplus, holding = total - reach - (amount - 1), [1] * (amount - 1)
    while surplus > 0:
        movable = [i for i in range(amount - 1) if holding[i] < reach]
        mass, left = sum([portions[i] for i in movable]), surplus
        for i in movable:
            more = min(reach - holding[i], max(1, left * portions[i] // mass), surplus)
            holding[i] = holding[i] + more
            surplus = surplus - more
    return np.array([reach] + holding)


def ragged_sizes(stream_key, amount, total, limit, slope):
    if amount == 2:
        one = jax.random.randint(stream_key, (), max(1, total - limit), min(limit, total - 1) + 1)
        return jnp.stack([one, total - one])
    sizes = jnp.asarray(profile(amount, total, limit, slope), jnp.int32)
    couples = (amount - 1) // 2
    giver, receiver = sizes[1:1 + 2 * couples:2], sizes[2:2 + 2 * couples:2]
    slack = jnp.minimum(giver - 1, limit - receiver)
    shifted = jax.random.randint(jax.random.fold_in(stream_key, 1), (couples,), 0, 1 << 20) % (slack + 1)
    sizes = sizes.at[1:1 + 2 * couples:2].set(giver - shifted).at[2:2 + 2 * couples:2].set(receiver + shifted)
    return sizes[jax.random.permutation(jax.random.fold_in(stream_key, 2), amount)]


def normal_values(stream_key, extent, width, most, cuts=(), kind=jnp.bfloat16):
    factor_of = levels(stream_key, extent, cuts, -0.22, 0.18) if cuts else 1.0
    array = jax.random.normal(stream_key, extent, jnp.float32) * width * factor_of
    return jnp.minimum(jnp.maximum(array, -most), most).astype(kind)


def setup_inputs(seed: int = 0) -> dict:
    key_of = jax.random.split(jax.random.key(seed), 6)
    hidden = normal_values(key_of[0], (TOKENS, D), 1.0, 6.0, ((0, 8),))
    head_weight = normal_values(key_of[1], (D, VOCAB), D ** -0.5, 0.09375, ((0, 8), (1, 64)))
    head_bias = normal_values(key_of[2], (VOCAB,), 0.5, 2.5, ((0, 64),), jnp.float32)
    rep_cotangent = normal_values(key_of[3], (SEQS, VOCAB), 1.0, 6.0, ((0, 8), (1, 64)), jnp.float32)
    lengths = ragged_sizes(key_of[4], SEQS, SEQS * LEN * 5 // 8, LEN, 2).astype(jnp.int32)
    return {"hidden": hidden, "head_weight": head_weight, "head_bias": head_bias, "rep_cotangent": rep_cotangent, "lengths": lengths}


def reference(hidden, head_weight, head_bias, rep_cotangent, lengths):
    block = D // N_DP
    logits = jnp.zeros((TOKENS, VOCAB), jnp.float32)
    for index in range(N_DP):
        part = jnp.dot(hidden[:, index * block:(index + 1) * block], head_weight[index * block:(index + 1) * block, :], preferred_element_type=jnp.float32).astype(jnp.bfloat16)
        logits = logits + lax.optimization_barrier(part).astype(jnp.float32)
    logits = logits + head_bias[None, :]
    positive = jnp.maximum(logits, 0.0)
    act = jnp.log1p(positive)
    grid = act.reshape(SEQS, LEN, VOCAB)
    live = (jnp.arange(LEN, dtype=jnp.int32)[None, :] < lengths[:, None]).astype(jnp.float32)[:, :, None]
    squared = grid * grid
    total = 1.0 + jnp.sum(live * squared * squared, axis=1)
    pooled = total ** 0.25 - 1.0
    term_mean = jnp.sum(pooled, axis=0) / SEQS
    grad_pooled = rep_cotangent + term_mean[None, :]
    factor = live * squared * grid * (total ** -0.75)[:, None, :] / (1.0 + positive.reshape(SEQS, LEN, VOCAB))
    grad_logits = (factor * grad_pooled[:, None, :]).reshape(TOKENS, VOCAB)
    bias_grad = jnp.sum(grad_logits, axis=0)
    grad_round = grad_logits.astype(jnp.bfloat16)
    weight_grad = jnp.dot(hidden.T, grad_round, preferred_element_type=jnp.float32)
    input_grad = jnp.dot(grad_round, head_weight.T, preferred_element_type=jnp.float32)
    return (pooled, term_mean, bias_grad, weight_grad, input_grad)
```

```python
import functools

import jax
import jax.numpy as jnp
from jax import lax
from jax.experimental import pallas as pl
from jax.experimental.pallas import tpu as pltpu
from jax.sharding import Mesh
from jax.sharding import PartitionSpec as P


F32 = jnp.float32
BF16 = jnp.bfloat16
I32 = jnp.int32

SEQS = 64
LEN = 16
TOKENS = SEQS * LEN
LIVE = SEQS * LEN * 5 // 8
HALF = LIVE // 2
LANES = 128
CUT = 256
BLOCK = 512
PACK = 176
EXTRA = 32

VMEM = functools.partial(pl.BlockSpec, memory_space=pltpu.VMEM)
SMEM = functools.partial(pl.BlockSpec, memory_space=pltpu.SMEM)


def call(body, outs, ins, flops=0, moved=0, scalars=1):
    return kernel(body, outs, ins, flops, moved, scalars)


def kernel(body, outs, ins, flops, moved, scalars):
    return pl.pallas_call(
        body,
        out_shape=outs,
        in_specs=[SMEM()] * scalars + [VMEM()] * (len(ins) - scalars),
        out_specs=jax.tree.map(lambda _: VMEM(), outs),
        cost_estimate=pl.CostEstimate(flops=flops, bytes_accessed=moved, transcendentals=0),
    )(*ins)


def iota(shape, dim):
    return lax.broadcasted_iota(I32, shape, dim)


def split(value):
    high = value.astype(BF16)
    return high, (value - high.astype(F32)).astype(BF16)


def dot(left, right, dims=((1,), (0,))):
    return lax.dot_general(left, right, (dims, ((), ())), preferred_element_type=F32)


def weights_body(at, w_ref, *outs):
    for m, out in enumerate(outs):
        start = pl.multiple_of((at[0] ^ m) * CUT, CUT)
        out[...] = w_ref[:, pl.ds(start, CUT)]


def packet_body(at, lengths, even_ref, odd_ref, cot_ref, out):
    row = iota((16, LANES), 0)
    lens = jnp.zeros((16, LANES), F32)
    for s in range(8):
        lens = jnp.where(row == s, lengths[s].astype(F32), lens)
    lens = lens.astype(BF16)
    for a in range(4):
        high, low = split(cot_ref[:, a * CUT : (a + 1) * CUT])
        pieces = []
        for part in (high.astype(F32), low.astype(F32)):
            pieces.append(jnp.concatenate([part[:, :LANES], part[:, LANES:]], axis=0).astype(BF16))
        for q, source in enumerate((even_ref, odd_ref)):
            k = 2 * a + q
            out[k, 0:128, :] = source[...]
            out[k, 128:144, :] = lens
            out[k, 144:160, :] = pieces[0]
            out[k, 160:176, :] = pieces[1]


def compact_body(at, got, out, cot_out, len_out):
    column = jnp.concatenate([got[k, 128:144, :].astype(F32)[0:8] for k in range(8)], axis=0)
    len_out[...] = column
    wide = jnp.broadcast_to(column[:, 0:1], (SEQS, TOKENS))
    seq = iota((SEQS, TOKENS), 0)
    token = iota((SEQS, TOKENS), 1)
    start = jnp.sum(jnp.where(seq < token // LEN, wide, 0.0), axis=0, keepdims=True)
    length = jnp.sum(jnp.where(seq == token // LEN, wide, 0.0), axis=0, keepdims=True)
    place = iota((1, TOKENS), 1) % LEN
    spot = jnp.where(place.astype(F32) < length, start.astype(I32) + place, -1)
    rows = iota((HALF, TOKENS), 0) + at[2] * HALF
    pick = jnp.where(jnp.broadcast_to(spot, (HALF, TOKENS)) == rows, 1.0, 0.0).astype(BF16)
    tokens = jnp.concatenate([got[k, 0:128, :] for k in range(8)], axis=0)
    chosen = dot(pick, tokens).astype(BF16)
    for j in range(16):
        out[j] = chosen
    for k in range(8):
        high = got[k, 144:160, :].astype(F32)
        low = got[k, 160:176, :].astype(F32)
        both = high + low
        cot_out[k * 8 : (k + 1) * 8, 0:LANES] = both[0:8]
        cot_out[k * 8 : (k + 1) * 8, LANES:CUT] = both[8:16]


def tables_body(at, len_ref, seg_ref, segt_ref, spread_ref):
    lens = len_ref[...]
    sub = iota((SEQS, LANES), 0)
    lane = iota((SEQS, LANES), 1)
    start_row = jnp.sum(jnp.where(sub < lane, lens, 0.0), axis=0, keepdims=True)
    len_row = jnp.sum(jnp.where(sub == lane, lens, 0.0), axis=0, keepdims=True)
    start_col = jnp.sum(
        jnp.where(lane < sub, jnp.broadcast_to(len_row, (SEQS, LANES)), 0.0), axis=1, keepdims=True
    )
    spot = iota((SEQS, LIVE), 1).astype(F32)
    first = jnp.broadcast_to(start_col, (SEQS, LIVE))
    last = jnp.broadcast_to(start_col + lens[:, 0:1], (SEQS, LIVE))
    seg_ref[...] = jnp.where((spot >= first) & (spot < last), 1.0, 0.0).astype(BF16)
    spot = iota((LIVE, LANES), 0).astype(F32)
    first = jnp.broadcast_to(start_row, (LIVE, LANES))
    last = jnp.broadcast_to(start_row + len_row, (LIVE, LANES))
    inside = (spot >= first) & (spot < last) & (iota((LIVE, LANES), 1) < SEQS)
    segt_ref[...] = jnp.where(inside, 1.0, 0.0).astype(BF16)
    row = iota((TOKENS, LANES), 0)
    lane = iota((TOKENS, LANES), 1)
    core = (row >> 9) ^ at[2]
    which = (((((row >> 4) & 1) * 4 + ((row >> 7) & 3)) * 2 + core) * 4) + ((row >> 5) & 3)
    per_row = jnp.broadcast_to(len_row, (TOKENS, LANES))
    start = jnp.sum(jnp.where(lane < which, per_row, 0.0), axis=1, keepdims=True)
    length = jnp.sum(jnp.where(lane == which, per_row, 0.0), axis=1, keepdims=True)
    place = (row[:, 0:1] & 15).astype(F32)
    spot = jnp.where(place < length, start + place, -1.0)
    target = iota((TOKENS, LIVE), 1).astype(F32)
    spread_ref[...] = jnp.where(jnp.broadcast_to(spot, (TOKENS, LIVE)) == target, 1.0, 0.0).astype(BF16)


def wide_rows(ref, block):
    return jnp.concatenate([ref[block * 4 + i] for i in range(4)], axis=1)


def logits_body(at, own, other, w0, w1, w2, w3, out):
    for hop, ref in enumerate((own, other)):
        total = jnp.zeros((HALF, CUT), F32)
        for m, w in enumerate((w0, w1, w2, w3)):
            total = total + dot(wide_rows(ref, at[0] ^ m), w[...])
        half = at[2] ^ hop
        out[pl.ds(pl.multiple_of(half * HALF, HALF), HALF), :] = total.astype(BF16)


def grads_body(at, mine, theirs, bias, cot, seg, segt, grad_out, x0, x1, x2, x3):
    logits = mine[...].astype(F32) + theirs[...].astype(F32) + bias[pl.ds(at[0], 1), :]
    positive = jnp.maximum(logits, 0.0)
    act = jnp.log1p(positive)
    cube = act * act * act
    high, low = split(cube * act)
    total = 1.0 + (dot(seg[...], high) + dot(seg[...], low))
    second = jnp.sqrt(total)
    fourth = jnp.sqrt(second)
    pooled = fourth - 1.0
    mean = jnp.sum(pooled, axis=0, keepdims=True) / SEQS
    pull = (cot[...] + mean) / (second * fourth)
    pad = jnp.zeros((LANES - SEQS, CUT), BF16)
    high, low = split(pull)
    spread = dot(segt[...], jnp.concatenate([high, pad], axis=0))
    spread = spread + dot(segt[...], jnp.concatenate([low, pad], axis=0))
    grad = spread * (cube / (1.0 + positive))
    bias_grad = jnp.sum(grad, axis=0, keepdims=True)
    grad_out[...] = grad.astype(BF16)
    m_high, m_low = split(mean)
    b_high, b_low = split(bias_grad)
    row = iota((16, CUT), 0)
    tail = jnp.zeros((16, CUT), F32)
    for i, v in enumerate((m_high, m_low, b_high, b_low)):
        tail = jnp.where(row == i, jnp.broadcast_to(v.astype(F32), (16, CUT)), tail)
    tail = tail.astype(BF16)
    for m, out in enumerate((x0, x1, x2, x3)):
        k = (at[0] ^ m) * 2 + at[1]
        mine8 = jnp.zeros((8, CUT), F32)
        for i in range(8):
            mine8 = jnp.where(k == i, pooled[i * 8 : (i + 1) * 8], mine8)
        high, low = split(mine8)
        out[0:16, :] = jnp.concatenate([high.astype(F32), low.astype(F32)], axis=0).astype(BF16)
        out[16:32, :] = tail


def weight_grad_body(at, own, other, grad, x0, x1, x2, x3, o0, o1, o2, o3):
    for m, (extra, out) in enumerate(zip((x0, x1, x2, x3), (o0, o1, o2, o3))):
        total = jnp.zeros((BLOCK, CUT), F32)
        for hop, ref in enumerate((own, other)):
            half = at[2] ^ hop
            part = grad[pl.ds(pl.multiple_of(half * HALF, HALF), HALF), :]
            total = total + dot(wide_rows(ref, at[0] ^ m), part, ((0,), (0,)))
        out[0:BLOCK, :] = total.astype(BF16)
        out[BLOCK : BLOCK + EXTRA, :] = extra[...]


def send_body(at, spread, grad, w0, w1, w2, w3, out):
    rows = dot(spread[TOKENS // 2 :, :], grad[...]).astype(BF16)
    for m, w in enumerate((w0, w1, w2, w3)):
        start = pl.multiple_of((at[0] ^ m) * BLOCK, BLOCK)
        out[:, pl.ds(start, BLOCK)] = dot(rows, w[...], ((1,), (1,))).astype(BF16)


def keep_body(at, spread, grad, w0, w1, w2, w3, got, out):
    rows = dot(spread[: TOKENS // 2, :], grad[...]).astype(BF16)
    for m, w in enumerate((w0, w1, w2, w3)):
        start = pl.multiple_of((at[0] ^ m) * BLOCK, BLOCK)
        part = dot(rows, w[...], ((1,), (1,)))
        out[:, pl.ds(start, BLOCK)] = (part + got[:, pl.ds(start, BLOCK)].astype(F32)).astype(BF16)


def plane_body(got, out):
    total = got[0].astype(F32)
    for i in range(1, 16):
        total = total + got[i].astype(F32)
    total = total.astype(BF16)
    for zh in range(2):
        for a in range(4):
            out[zh * 4 + a] = total[zh * 16 : (zh + 1) * 16, a * BLOCK : (a + 1) * BLOCK]


def last_body(got, out):
    total = got[0].astype(F32)
    for i in range(1, 8):
        total = total + got[i].astype(F32)
    out[...] = total


def unpack_body(at, p0, p1, p2, p3, weight_out, pooled_out, mean_out, bias_out):
    for m, piece in enumerate((p0, p1, p2, p3)):
        columns = pl.ds(pl.multiple_of((at[0] ^ m) * CUT, CUT), CUT)
        weight_out[:, columns] = piece[0:BLOCK, :].astype(F32)
        extra = piece[BLOCK : BLOCK + EXTRA, :].astype(F32)
        pooled_out[:, columns] = extra[0:8] + extra[8:16]
        mean_out[:, columns] = extra[16:17] + extra[17:18]
        bias_out[:, columns] = extra[18:19] + extra[19:20]


def pack(at, lengths, hidden, rep_cotangent):
    return pl.pallas_call(
        packet_body,
        grid_spec=pltpu.PrefetchScalarGridSpec(
            num_scalar_prefetch=2,
            grid=(1,),
            in_specs=[
                pl.BlockSpec((128, LANES), lambda i, at, n: (0, at[4])),
                pl.BlockSpec((128, LANES), lambda i, at, n: (0, at[4] + 4)),
                pl.BlockSpec((8, 1024), lambda i, at, n: (0, 0)),
            ],
            out_specs=pl.BlockSpec((8, PACK, LANES), lambda i, at, n: (0, 0, 0)),
        ),
        out_shape=shape((8, PACK, LANES)),
        name="packet",
    )(at, lengths, hidden, hidden, rep_cotangent)


def shape(dims, kind=BF16):
    return jax.ShapeDtypeStruct(dims, kind)


def per_device(hidden, head_weight, head_bias, rep_cotangent, lengths):
    a, q, c = lax.axis_index("zq"), lax.axis_index("zp"), lax.axis_index("c")
    j = lax.axis_index("y") * 4 + lax.axis_index("x")
    spot = (2 * (j // 4)) * 4 + j % 4
    at = jnp.stack([a, q, c, j, spot, spot, spot, spot]).astype(I32)

    def swap(value, axis, size, m):
        return lax.ppermute(value, axis, [(i, i ^ m) for i in range(size)])

    def trade(value, axes):
        return lax.all_to_all(value, axes, 0, 0, tiled=True)

    w = call(weights_body, [shape((BLOCK, CUT))] * 4, [at, head_weight])
    w = [w[0]] + [swap(w[m], "zq", 4, m) for m in (1, 2, 3)]

    packets = pack(at, lengths, hidden, rep_cotangent)
    got = trade(packets, ("zq", "zp"))
    rows, cot, lens = call(
        compact_body,
        [shape((16, HALF, LANES)), shape((SEQS, CUT), F32), shape((SEQS, LANES), F32)],
        [at, got],
    )
    own = trade(rows, ("y", "x"))
    other = swap(own, "c", 2, 1)
    seg, segt, spread = call(
        tables_body,
        [shape((SEQS, LIVE)), shape((LIVE, LANES)), shape((TOKENS, LIVE))],
        [at, lens],
        flops=10_000_000,
        moved=2_000_000,
    )
    mine = call(
        logits_body, shape((LIVE, CUT)), [at, own, other, *w], 2 * LIVE * 2048 * CUT, 4 << 20
    )
    theirs = swap(mine, "zp", 2, 1)
    grad, *extra = call(
        grads_body,
        [shape((LIVE, CUT))] + [shape((EXTRA, CUT))] * 4,
        [at, mine, theirs, head_bias.reshape(4, CUT), cot, seg, segt],
    )
    send = call(
        send_body, shape((512, 2048)), [at, spread, grad, *w], 2 * 512 * 2048 * CUT, 4 << 20
    )
    came = swap(send, "c", 2, 1)
    pieces = call(
        weight_grad_body,
        [shape((BLOCK + EXTRA, CUT))] * 4,
        [at, own, other, grad, *extra],
        2 * LIVE * 2048 * CUT,
        4 << 20,
    )
    pieces = [pieces[0]] + [swap(pieces[m], "zq", 4, m) for m in (1, 2, 3)]
    kept = call(
        keep_body, shape((512, 2048)), [at, spread, grad, *w, came], 2 * 512 * 2048 * CUT, 6 << 20
    )
    plane = trade(kept.reshape(16, 32, 2048), ("y", "x"))
    column = call(plane_body, shape((8, 16, BLOCK)), [plane], scalars=0)
    column = trade(column, ("zh", "zq"))
    input_grad = call(last_body, shape((16, BLOCK), F32), [column], scalars=0)
    weight_grad, pooled, mean, bias_grad = call(
        unpack_body,
        [shape((BLOCK, 1024), F32), shape((8, 1024), F32), shape((1, 1024), F32), shape((1, 1024), F32)],
        [at, *pieces],
    )
    return pooled, mean.reshape(1024), bias_grad.reshape(1024), weight_grad, input_grad


def solution(mesh):
    fine = Mesh(mesh.devices.reshape(2, 4, 2, 4, 2, 4), ("zh", "y", "c", "zq", "zp", "x"))
    dp = ("zq", "zp")
    columns = ("zh", "y", "c", "x")

    return jax.shard_map(
        per_device,
        mesh=fine,
        in_specs=(P(dp, None), P(dp, columns), P(columns), P(dp, columns), P(dp)),
        out_specs=(P(dp, columns), P(columns), P(columns), P(dp, columns), P(columns, dp)),
        check_vma=False,
    )
```

```python
import functools

import jax
import jax.numpy as jnp
from jax import lax
from jax.experimental import pallas as pl
from jax.experimental.pallas import tpu as pltpu
from jax.sharding import Mesh
from jax.sharding import PartitionSpec as P


F32 = jnp.float32
BF16 = jnp.bfloat16
I32 = jnp.int32

SEQS = 64
LEN = 16
TOKENS = SEQS * LEN
LIVE = SEQS * LEN * 5 // 8
HALF = LIVE // 2
LANES = 128
CUT = 256
BLOCK = 512
PACK = 176
EXTRA = 32

VMEM = functools.partial(pl.BlockSpec, memory_space=pltpu.VMEM)
SMEM = functools.partial(pl.BlockSpec, memory_space=pltpu.SMEM)


def call(body, outs, ins, flops=0, moved=0, name=None):
    return kernel(body, outs, ins, flops, moved, name)


def kernel(body, outs, ins, flops, moved, name):
    ins = [pltpu.with_memory_space_constraint(x, pltpu.VMEM) for x in ins]
    return pl.pallas_call(
        body,
        out_shape=jax.tree.map(lambda o: pltpu.VMEM(o.shape, o.dtype), outs) if name in KEEP else outs,
        in_specs=[VMEM()] * len(ins),
        out_specs=jax.tree.map(lambda _: VMEM(), outs),
        compiler_params=pltpu.CompilerParams(vmem_limit_bytes=20 << 20),
        cost_estimate=pl.CostEstimate(flops=flops, bytes_accessed=moved, transcendentals=0),
    )(*ins)


KEEP = ("weights", "compact", "logits", "grads", "send", "keep", "plane", "weight_grad", "tables")


def home():
    return lax.axis_index("zq"), lax.axis_index("zp"), lax.axis_index("c")


def iota(shape, dim):
    return lax.broadcasted_iota(I32, shape, dim)


def split(value):
    high = value.astype(BF16)
    return high, (value - high.astype(F32)).astype(BF16)


def dot(left, right, dims=((1,), (0,))):
    return lax.dot_general(left, right, (dims, ((), ())), preferred_element_type=F32)


def weights_body(w_ref, o0, o1, o2, o3, sems):
    at = home()
    copies = []
    for m, out in enumerate((o0, o1, o2, o3)):
        start = pl.multiple_of((at[0] ^ m) * CUT, CUT)
        copies.append(pltpu.make_async_copy(w_ref.at[:, pl.ds(start, CUT)], out, sems.at[m]))
        copies[-1].start()
    for copy in copies:
        copy.wait()


def packet_body(lengths, hidden_ref, cot_hbm, out, even_ref, odd_ref, cot_ref, sems):
    spot = (8 * lax.axis_index("y") + lax.axis_index("x")) * LANES
    copies = []
    for i, ref in enumerate((even_ref, odd_ref)):
        start = pl.multiple_of(spot + i * BLOCK, LANES)
        copies.append(pltpu.make_async_copy(hidden_ref.at[:, pl.ds(start, LANES)], ref, sems.at[i]))
    copies.append(pltpu.make_async_copy(cot_hbm, cot_ref, sems.at[2]))
    for copy in copies:
        copy.start()
    for copy in copies:
        copy.wait()
    row = iota((16, LANES), 0)
    lens = jnp.zeros((16, LANES), F32)
    for s in range(8):
        lens = jnp.where(row == s, lengths[s].astype(F32), lens)
    lens = lens.astype(BF16)
    for a in range(4):
        high, low = split(cot_ref[:, a * CUT : (a + 1) * CUT])
        pieces = []
        for part in (high.astype(F32), low.astype(F32)):
            pieces.append(jnp.concatenate([part[:, :LANES], part[:, LANES:]], axis=0).astype(BF16))
        for q, source in enumerate((even_ref, odd_ref)):
            k = 2 * a + q
            out[k, 0:128, :] = source[...]
            out[k, 128:144, :] = lens
            out[k, 144:160, :] = pieces[0]
            out[k, 160:176, :] = pieces[1]


def compact_body(got, out, cot_out, len_out):
    at = home()
    column = jnp.concatenate([got[k, 128:144, :].astype(F32)[0:8] for k in range(8)], axis=0)
    len_out[...] = column
    wide = jnp.broadcast_to(column[:, 0:1], (SEQS, TOKENS))
    seq = iota((SEQS, TOKENS), 0)
    token = iota((SEQS, TOKENS), 1)
    start = jnp.sum(jnp.where(seq < token // LEN, wide, 0.0), axis=0, keepdims=True)
    length = jnp.sum(jnp.where(seq == token // LEN, wide, 0.0), axis=0, keepdims=True)
    place = iota((1, TOKENS), 1) % LEN
    spot = jnp.where(place.astype(F32) < length, start.astype(I32) + place, -1)
    rows = iota((HALF, TOKENS), 0) + at[2] * HALF
    pick = jnp.where(jnp.broadcast_to(spot, (HALF, TOKENS)) == rows, 1.0, 0.0).astype(BF16)
    tokens = jnp.concatenate([got[k, 0:128, :] for k in range(8)], axis=0)
    chosen = dot(pick, tokens).astype(BF16)
    for j in range(16):
        out[j] = chosen
    for k in range(8):
        high = got[k, 144:160, :].astype(F32)
        low = got[k, 160:176, :].astype(F32)
        both = high + low
        cot_out[k * 8 : (k + 1) * 8, 0:LANES] = both[0:8]
        cot_out[k * 8 : (k + 1) * 8, LANES:CUT] = both[8:16]


def tables_body(len_ref, seg_ref, segt_ref, spread_ref):
    at = home()
    lens = len_ref[...]
    sub = iota((SEQS, LANES), 0)
    lane = iota((SEQS, LANES), 1)
    start_row = jnp.sum(jnp.where(sub < lane, lens, 0.0), axis=0, keepdims=True)
    len_row = jnp.sum(jnp.where(sub == lane, lens, 0.0), axis=0, keepdims=True)
    start_col = jnp.sum(
        jnp.where(lane < sub, jnp.broadcast_to(len_row, (SEQS, LANES)), 0.0), axis=1, keepdims=True
    )
    spot = iota((SEQS, LIVE), 1).astype(F32)
    first = jnp.broadcast_to(start_col, (SEQS, LIVE))
    last = jnp.broadcast_to(start_col + lens[:, 0:1], (SEQS, LIVE))
    seg_ref[...] = jnp.where((spot >= first) & (spot < last), 1.0, 0.0).astype(BF16)
    spot = iota((LIVE, LANES), 0).astype(F32)
    first = jnp.broadcast_to(start_row, (LIVE, LANES))
    last = jnp.broadcast_to(start_row + len_row, (LIVE, LANES))
    inside = (spot >= first) & (spot < last) & (iota((LIVE, LANES), 1) < SEQS)
    segt_ref[...] = jnp.where(inside, 1.0, 0.0).astype(BF16)
    row = iota((TOKENS, LANES), 0)
    lane = iota((TOKENS, LANES), 1)
    core = (row >> 9) ^ at[2]
    which = (((((row >> 4) & 1) * 4 + ((row >> 7) & 3)) * 2 + core) * 4) + ((row >> 5) & 3)
    per_row = jnp.broadcast_to(len_row, (TOKENS, LANES))
    start = jnp.sum(jnp.where(lane < which, per_row, 0.0), axis=1, keepdims=True)
    length = jnp.sum(jnp.where(lane == which, per_row, 0.0), axis=1, keepdims=True)
    place = (row[:, 0:1] & 15).astype(F32)
    spot = jnp.where(place < length, start + place, -1.0)
    target = iota((TOKENS, LIVE), 1).astype(F32)
    spread_ref[...] = jnp.where(jnp.broadcast_to(spot, (TOKENS, LIVE)) == target, 1.0, 0.0).astype(BF16)


def wide_rows(ref, block):
    return jnp.concatenate([ref[block * 4 + i] for i in range(4)], axis=1)


def logits_body(own, other, w0, w1, w2, w3, out):
    at = home()
    for hop, ref in enumerate((own, other)):
        total = jnp.zeros((HALF, CUT), F32)
        for m, w in enumerate((w0, w1, w2, w3)):
            total = total + dot(wide_rows(ref, at[0] ^ m), w[...])
        half = at[2] ^ hop
        out[pl.ds(pl.multiple_of(half * HALF, HALF), HALF), :] = total.astype(BF16)


def grads_body(mine, theirs, bias, cot, seg, segt, grad_out, x0, x1, x2, x3):
    at = home()
    logits = mine[...].astype(F32) + theirs[...].astype(F32) + bias[pl.ds(at[0], 1), :]
    positive = jnp.maximum(logits, 0.0)
    act = jnp.log1p(positive)
    cube = act * act * act
    high, low = split(cube * act)
    total = 1.0 + (dot(seg[...], high) + dot(seg[...], low))
    second = jnp.sqrt(total)
    fourth = jnp.sqrt(second)
    pooled = fourth - 1.0
    mean = jnp.sum(pooled, axis=0, keepdims=True) / SEQS
    pull = (cot[...] + mean) / (second * fourth)
    pad = jnp.zeros((LANES - SEQS, CUT), BF16)
    high, low = split(pull)
    spread = dot(segt[...], jnp.concatenate([high, pad], axis=0))
    spread = spread + dot(segt[...], jnp.concatenate([low, pad], axis=0))
    grad = spread * (cube / (1.0 + positive))
    bias_grad = jnp.sum(grad, axis=0, keepdims=True)
    grad_out[...] = grad.astype(BF16)
    m_high, m_low = split(mean)
    b_high, b_low = split(bias_grad)
    row = iota((16, CUT), 0)
    tail = jnp.zeros((16, CUT), F32)
    for i, v in enumerate((m_high, m_low, b_high, b_low)):
        tail = jnp.where(row == i, jnp.broadcast_to(v.astype(F32), (16, CUT)), tail)
    tail = tail.astype(BF16)
    for m, out in enumerate((x0, x1, x2, x3)):
        k = (at[0] ^ m) * 2 + at[1]
        mine8 = jnp.zeros((8, CUT), F32)
        for i in range(8):
            mine8 = jnp.where(k == i, pooled[i * 8 : (i + 1) * 8], mine8)
        high, low = split(mine8)
        out[0:16, :] = jnp.concatenate([high.astype(F32), low.astype(F32)], axis=0).astype(BF16)
        out[16:32, :] = tail


def weight_grad_body(own, other, grad, x0, x1, x2, x3, o0, o1, o2, o3):
    at = home()
    for m, (extra, out) in enumerate(zip((x0, x1, x2, x3), (o0, o1, o2, o3))):
        total = jnp.zeros((BLOCK, CUT), F32)
        for hop, ref in enumerate((own, other)):
            half = at[2] ^ hop
            part = grad[pl.ds(pl.multiple_of(half * HALF, HALF), HALF), :]
            total = total + dot(wide_rows(ref, at[0] ^ m), part, ((0,), (0,)))
        out[0:BLOCK, :] = total.astype(BF16)
        out[BLOCK : BLOCK + EXTRA, :] = extra[...]


def send_body(spread, grad, w0, w1, w2, w3, out):
    at = home()
    rows = dot(spread[TOKENS // 2 :, :], grad[...]).astype(BF16)
    for m, w in enumerate((w0, w1, w2, w3)):
        start = pl.multiple_of((at[0] ^ m) * BLOCK, BLOCK)
        out[:, pl.ds(start, BLOCK)] = dot(rows, w[...], ((1,), (1,))).astype(BF16)


def keep_body(spread, grad, w0, w1, w2, w3, got, out):
    at = home()
    rows = dot(spread[: TOKENS // 2, :], grad[...]).astype(BF16)
    for m, w in enumerate((w0, w1, w2, w3)):
        start = pl.multiple_of((at[0] ^ m) * BLOCK, BLOCK)
        part = dot(rows, w[...], ((1,), (1,)))
        out[:, pl.ds(start, BLOCK)] = (part + got[:, pl.ds(start, BLOCK)].astype(F32)).astype(BF16)


def plane_body(got, out):
    total = got[0].astype(F32)
    for i in range(1, 16):
        total = total + got[i].astype(F32)
    total = total.astype(BF16)
    for zh in range(2):
        for a in range(4):
            out[zh * 4 + a] = total[zh * 16 : (zh + 1) * 16, a * BLOCK : (a + 1) * BLOCK]


def last_body(got, out):
    total = got[0].astype(F32)
    for i in range(1, 8):
        total = total + got[i].astype(F32)
    out[...] = total


def unpack_body(p0, p1, p2, p3, weight_out, pooled_out, mean_out, bias_out):
    at = home()
    for m, piece in enumerate((p0, p1, p2, p3)):
        columns = pl.ds(pl.multiple_of((at[0] ^ m) * CUT, CUT), CUT)
        weight_out[:, columns] = piece[0:BLOCK, :].astype(F32)
        extra = piece[BLOCK : BLOCK + EXTRA, :].astype(F32)
        pooled_out[:, columns] = extra[0:8] + extra[8:16]
        mean_out[:, columns] = extra[16:17] + extra[17:18]
        bias_out[:, columns] = extra[18:19] + extra[19:20]


def pack(lengths, hidden, rep_cotangent):
    return pl.pallas_call(
        packet_body,
        out_shape=pltpu.VMEM((8, PACK, LANES), BF16),
        in_specs=[SMEM(), pl.BlockSpec(memory_space=pltpu.HBM), pl.BlockSpec(memory_space=pltpu.HBM)],
        out_specs=VMEM(),
        scratch_shapes=[
            pltpu.VMEM((128, LANES), BF16),
            pltpu.VMEM((128, LANES), BF16),
            pltpu.VMEM((8, 1024), F32),
            pltpu.SemaphoreType.DMA((3,)),
        ],
        compiler_params=pltpu.CompilerParams(vmem_limit_bytes=8 << 20),
        name="packet",
    )(lengths, hidden, rep_cotangent)


def cut(head_weight):
    return pl.pallas_call(
        weights_body,
        out_shape=[pltpu.VMEM((BLOCK, CUT), BF16)] * 4,
        in_specs=[pl.BlockSpec(memory_space=pltpu.HBM)],
        out_specs=[VMEM()] * 4,
        scratch_shapes=[pltpu.SemaphoreType.DMA((4,))],
        compiler_params=pltpu.CompilerParams(vmem_limit_bytes=8 << 20),
        name="weights",
    )(head_weight)


def shape(dims, kind=BF16):
    return jax.ShapeDtypeStruct(dims, kind)


def per_device(hidden, head_weight, head_bias, rep_cotangent, lengths):
    def swap(value, axis, size, m):
        return lax.ppermute(value, axis, [(i, i ^ m) for i in range(size)])

    def trade(value, axes):
        return lax.all_to_all(value, axes, 0, 0, tiled=True)

    w = cut(head_weight)
    w = [w[0]] + [swap(w[m], "zq", 4, m) for m in (1, 2, 3)]

    packets = pack(lengths, hidden, rep_cotangent)
    got = trade(packets, ("zq", "zp"))
    rows, cot, lens = call(
        compact_body,
        [shape((16, HALF, LANES)), shape((SEQS, CUT), F32), shape((SEQS, LANES), F32)],
        [got],
        name="compact",
    )
    own = trade(rows, ("y", "x"))
    other = swap(own, "c", 2, 1)
    seg, segt, spread = call(
        tables_body,
        [shape((SEQS, LIVE)), shape((LIVE, LANES)), shape((TOKENS, LIVE))],
        [lens],
        flops=10_000_000,
        moved=2_000_000,
        name="tables",
    )
    mine = call(
        logits_body, shape((LIVE, CUT)), [own, other, *w], 2 * LIVE * 2048 * CUT, 4 << 20, name="logits"
    )
    theirs = swap(mine, "zp", 2, 1)
    grad, *extra = call(
        grads_body,
        [shape((LIVE, CUT))] + [shape((EXTRA, CUT))] * 4,
        [mine, theirs, head_bias.reshape(4, CUT), cot, seg, segt],
        name="grads",
    )
    send = call(
        send_body, shape((512, 2048)), [spread, grad, *w], 2 * 512 * 2048 * CUT, 4 << 20, name="send"
    )
    came = swap(send, "c", 2, 1)
    pieces = call(
        weight_grad_body,
        [shape((BLOCK + EXTRA, CUT))] * 4,
        [own, other, grad, *extra],
        2 * LIVE * 2048 * CUT,
        4 << 20,
        name="weight_grad",
    )
    pieces = [pieces[0]] + [swap(pieces[m], "zq", 4, m) for m in (1, 2, 3)]
    kept = call(
        keep_body, shape((512, 2048)), [spread, grad, *w, came], 2 * 512 * 2048 * CUT, 6 << 20, name="keep"
    )
    plane = trade(kept.reshape(16, 32, 2048), ("y", "x"))
    column = call(plane_body, shape((8, 16, BLOCK)), [plane], name="plane")
    column = trade(column, ("zh", "zq"))
    input_grad = call(last_body, shape((16, BLOCK), F32), [column], name="last")
    weight_grad, pooled, mean, bias_grad = call(
        unpack_body,
        [shape((BLOCK, 1024), F32), shape((8, 1024), F32), shape((1, 1024), F32), shape((1, 1024), F32)],
        [*pieces],
        name="unpack",
    )
    return pooled, mean.reshape(1024), bias_grad.reshape(1024), weight_grad, input_grad


def solution(mesh):
    fine = Mesh(mesh.devices.reshape(2, 4, 2, 4, 2, 4), ("zh", "y", "c", "zq", "zp", "x"))
    dp = ("zq", "zp")
    columns = ("zh", "y", "c", "x")

    return jax.shard_map(
        per_device,
        mesh=fine,
        in_specs=(P(dp, None), P(dp, columns), P(columns), P(dp, columns), P(dp)),
        out_specs=(P(dp, columns), P(columns), P(columns), P(dp, columns), P(columns, dp)),
        check_vma=False,
    )
```

```python
import functools

import jax
import jax.numpy as jnp
from jax import lax
from jax.experimental import pallas as pl
from jax.experimental.pallas import tpu as pltpu
from jax.sharding import Mesh
from jax.sharding import PartitionSpec as P


F32 = jnp.float32
BF16 = jnp.bfloat16
I32 = jnp.int32

SEQS = 64
LEN = 16
TOKENS = SEQS * LEN
LIVE = SEQS * LEN * 5 // 8
HALF = LIVE // 2
LANES = 128
CUT = 256
BLOCK = 512
PACK = 96
EXTRA = 32

VMEM = functools.partial(pl.BlockSpec, memory_space=pltpu.VMEM)
SMEM = functools.partial(pl.BlockSpec, memory_space=pltpu.SMEM)


def call(body, outs, ins, flops=0, moved=0, name=None):
    return kernel(body, outs, ins, flops, moved, name)


def kernel(body, outs, ins, flops, moved, name):
    ins = [pltpu.with_memory_space_constraint(x, pltpu.VMEM) for x in ins]
    place = pltpu.VMEM if name in KEEP else pltpu.HBM if name in LEAVE else None
    return pl.pallas_call(
        body,
        out_shape=jax.tree.map(lambda o: place(o.shape, o.dtype), outs) if place else outs,
        in_specs=[VMEM()] * len(ins),
        out_specs=jax.tree.map(lambda _: VMEM(), outs),
        compiler_params=pltpu.CompilerParams(vmem_limit_bytes=20 << 20),
        cost_estimate=pl.CostEstimate(flops=flops, bytes_accessed=moved, transcendentals=0),
    )(*ins)


KEEP = ("compact", "logits", "grads", "halves", "plane", "tables")
LEAVE = ("input",)


def home():
    return lax.axis_index("zq"), lax.axis_index("zp"), lax.axis_index("c")


def iota(shape, dim):
    return lax.broadcasted_iota(I32, shape, dim)


def split(value):
    high = value.astype(BF16)
    return high, (value - high.astype(F32)).astype(BF16)


def dot(left, right, dims=((1,), (0,))):
    return lax.dot_general(left, right, (dims, ((), ())), preferred_element_type=F32)


def weights_body(w_ref, o0, o1, o2, o3, sems):
    at = home()
    copies = []
    for m, out in enumerate((o0, o1, o2, o3)):
        start = pl.multiple_of((at[0] ^ m) * CUT, CUT)
        copies.append(pltpu.make_async_copy(w_ref.at[:, pl.ds(start, CUT)], out, sems.at[m]))
        copies[-1].start()
    for copy in copies:
        copy.wait()


def packet_body(lengths, hidden_ref, cot_hbm, out, near_ref, far_ref, cot_ref, sems):
    spot = (4 * lax.axis_index("y") + lax.axis_index("x")) * LANES
    copies = []
    for i, ref in enumerate((near_ref, far_ref)):
        start = pl.multiple_of(spot + i * 2048, LANES)
        copies.append(pltpu.make_async_copy(hidden_ref.at[:, pl.ds(start, LANES)], ref, sems.at[i]))
    copies.append(pltpu.make_async_copy(cot_hbm, cot_ref, sems.at[2]))
    for copy in copies:
        copy.start()
    for copy in copies:
        copy.wait()
    row = iota((16, LANES), 0)
    lens = jnp.zeros((16, LANES), F32)
    for s in range(8):
        lens = jnp.where(row == s, lengths[s].astype(F32), lens)
    lens = lens.astype(BF16)
    first = iota((64, LANES), 1) < 64
    low_core = lax.axis_index("c") == 0
    folded = []
    for ref in (near_ref, far_ref):
        top, bottom = ref[0:64, :].astype(F32), ref[64:128, :].astype(F32)
        zero = jnp.where(first, top, pltpu.roll(bottom, 64, 1))
        one = jnp.where(first, pltpu.roll(top, 64, 1), bottom)
        folded.append(jnp.where(low_core, zero, one).astype(BF16))
    for a in range(4):
        part = cot_ref[:, a * CUT : (a + 1) * CUT]
        part = jnp.concatenate([part[:, :LANES], part[:, LANES:]], axis=0).astype(BF16)
        for q in range(2):
            k = 4 * q + a
            out[k, 0:64, :] = folded[q]
            out[k, 64:80, :] = lens
            out[k, 80:96, :] = part


def compact_body(got, out, cot_out, len_out):
    column = jnp.concatenate([got[k, 64:80, :].astype(F32)[0:8] for k in range(8)], axis=0)
    len_out[...] = column
    wide = jnp.broadcast_to(column[:, 0:1], (SEQS, TOKENS // 2))
    seq = iota((SEQS, TOKENS // 2), 0)
    index = iota((SEQS, TOKENS // 2), 1)
    tokens = jnp.concatenate([got[k, 0:64, :] for k in range(8)], axis=0)
    rows = iota((LIVE, TOKENS // 2), 0)
    chosen = []
    for half in range(2):
        owner = (index // 64) * 8 + half * 4 + (index % 64) // LEN
        start = jnp.sum(jnp.where(seq < owner, wide, 0.0), axis=0, keepdims=True)
        length = jnp.sum(jnp.where(seq == owner, wide, 0.0), axis=0, keepdims=True)
        place = iota((1, TOKENS // 2), 1) % LEN
        spot = jnp.where(place.astype(F32) < length, start.astype(I32) + place, -1)
        pick = jnp.where(jnp.broadcast_to(spot, rows.shape) == rows, 1.0, 0.0).astype(BF16)
        chosen.append(dot(pick, tokens))
    first = iota((HALF, LANES), 1) < 64
    early = chosen[0][:HALF] + pltpu.roll(chosen[1][:HALF], 64, 1)
    late = pltpu.roll(chosen[0][HALF:], 64, 1) + chosen[1][HALF:]
    folded = jnp.where(first, early, late).astype(BF16)
    for j in range(16):
        out[j] = folded
    for k in range(8):
        cot = got[k, 80:96, :].astype(F32)
        cot_out[k * 8 : (k + 1) * 8, 0:LANES] = cot[0:8]
        cot_out[k * 8 : (k + 1) * 8, LANES:CUT] = cot[8:16]


def tables_body(len_ref, seg_ref, segt_ref, spread_ref):
    lens = len_ref[...]
    sub = iota((SEQS, LANES), 0)
    lane = iota((SEQS, LANES), 1)
    start_row = jnp.sum(jnp.where(sub < lane, lens, 0.0), axis=0, keepdims=True)
    len_row = jnp.sum(jnp.where(sub == lane, lens, 0.0), axis=0, keepdims=True)
    start_col = jnp.sum(
        jnp.where(lane < sub, jnp.broadcast_to(len_row, (SEQS, LANES)), 0.0), axis=1, keepdims=True
    )
    spot = iota((SEQS, LIVE), 1).astype(F32)
    first = jnp.broadcast_to(start_col, (SEQS, LIVE))
    last = jnp.broadcast_to(start_col + lens[:, 0:1], (SEQS, LIVE))
    seg_ref[...] = jnp.where((spot >= first) & (spot < last), 1.0, 0.0).astype(BF16)
    spot = iota((LIVE, LANES), 0).astype(F32)
    first = jnp.broadcast_to(start_row, (LIVE, LANES))
    last = jnp.broadcast_to(start_row + len_row, (LIVE, LANES))
    inside = (spot >= first) & (spot < last) & (iota((LIVE, LANES), 1) < SEQS)
    segt_ref[...] = jnp.where(inside, 1.0, 0.0).astype(BF16)
    row = iota((TOKENS, LANES), 0)
    lane = iota((TOKENS, LANES), 1)
    which = ((((row >> 5) & 1) * 4 + (row >> 8)) * 2 + ((row >> 4) & 1)) * 4 + ((row >> 6) & 3)
    per_row = jnp.broadcast_to(len_row, (TOKENS, LANES))
    start = jnp.sum(jnp.where(lane < which, per_row, 0.0), axis=1, keepdims=True)
    length = jnp.sum(jnp.where(lane == which, per_row, 0.0), axis=1, keepdims=True)
    place = (row[:, 0:1] & 15).astype(F32)
    spot = jnp.where(place < length, start + place, -1.0)
    target = iota((TOKENS, LIVE), 1).astype(F32)
    spread_ref[...] = jnp.where(jnp.broadcast_to(spot, (TOKENS, LIVE)) == target, 1.0, 0.0).astype(BF16)


def logits_body(own, other, w0, w1, w2, w3, out, rows_out):
    at = home()

    def unfold(low, high):
        first = iota((HALF, LANES), 1) < 64
        for j in range(16):
            left, right = low[j], high[j]
            columns = pl.ds((j % 4) * LANES, LANES)
            rows_out[j // 4, 0:HALF, columns] = jnp.where(first, left, pltpu.roll(right, 64, 1))
            rows_out[j // 4, HALF:LIVE, columns] = jnp.where(first, pltpu.roll(left, 64, 1), right)

    @pl.when(at[2] == 0)
    def _():
        unfold(own, other)

    @pl.when(at[2] == 1)
    def _():
        unfold(other, own)

    total = jnp.zeros((LIVE, CUT), F32)
    for m, w in enumerate((w0, w1, w2, w3)):
        total = total + dot(rows_out[at[0] ^ m], w[...])
    out[...] = total.astype(BF16)


def grads_body(mine, theirs, bias, cot, seg, segt, grad_out, x0, x1, x2, x3):
    at = home()
    logits = mine[...].astype(F32) + theirs[...].astype(F32) + bias[pl.ds(at[0], 1), :]
    positive = jnp.maximum(logits, 0.0)
    act = jnp.log1p(positive)
    cube = act * act * act
    high, low = split(cube * act)
    total = 1.0 + (dot(seg[...], high) + dot(seg[...], low))
    second = jnp.sqrt(total)
    fourth = jnp.sqrt(second)
    pooled = fourth - 1.0
    mean = jnp.sum(pooled, axis=0, keepdims=True) / SEQS
    pull = (cot[...] + mean) / (second * fourth)
    pad = jnp.zeros((LANES - SEQS, CUT), BF16)
    high, low = split(pull)
    spread = dot(segt[...], jnp.concatenate([high, pad], axis=0))
    spread = spread + dot(segt[...], jnp.concatenate([low, pad], axis=0))
    grad = spread * (cube / (1.0 + positive))
    bias_grad = jnp.sum(grad, axis=0, keepdims=True)
    grad_out[...] = grad.astype(BF16)
    m_high, m_low = split(mean)
    b_high, b_low = split(bias_grad)
    row = iota((16, CUT), 0)
    tail = jnp.zeros((16, CUT), F32)
    for i, v in enumerate((m_high, m_low, b_high, b_low)):
        tail = jnp.where(row == i, jnp.broadcast_to(v.astype(F32), (16, CUT)), tail)
    tail = tail.astype(BF16)
    for m, out in enumerate((x0, x1, x2, x3)):
        k = at[1] * 4 + (at[0] ^ m)
        mine8 = jnp.zeros((8, CUT), F32)
        for i in range(8):
            mine8 = jnp.where(k == i, pooled[i * 8 : (i + 1) * 8], mine8)
        high, low = split(mine8)
        out[0:16, :] = jnp.concatenate([high.astype(F32), low.astype(F32)], axis=0).astype(BF16)
        out[16:32, :] = tail


def weight_grad_body(rows, grad, x0, x1, x2, x3, o0, o1, o2, o3):
    at = home()
    for m, (extra, out) in enumerate(zip((x0, x1, x2, x3), (o0, o1, o2, o3))):
        out[0:BLOCK, :] = dot(rows[at[0] ^ m], grad[...], ((0,), (0,))).astype(BF16)
        out[BLOCK : BLOCK + EXTRA, :] = extra[...]


def halves_body(w0, w1, w2, w3, out):
    start = pl.multiple_of((1 - lax.axis_index("c")) * CUT, CUT)
    for m, w in enumerate((w0, w1, w2, w3)):
        out[m] = w[pl.ds(start, CUT), :]


def input_body(spread, grad, partner, w0, w1, w2, w3, half, out):
    at = home()
    start = pl.multiple_of(at[2] * CUT, CUT)
    mine = dot(spread[...], grad[...]).astype(BF16)
    theirs = dot(spread[...], partner[...]).astype(BF16)
    for m, w in enumerate((w0, w1, w2, w3)):
        total = dot(mine, w[pl.ds(start, CUT), :], ((1,), (1,)))
        total = total + dot(theirs, half[m], ((1,), (1,)))
        out[:, pl.ds(pl.multiple_of((at[0] ^ m) * CUT, CUT), CUT)] = total.astype(BF16)


def plane_body(got, out):
    total = got[0].astype(F32)
    for i in range(1, 16):
        total = total + got[i].astype(F32)
    total = total.astype(BF16)
    for zh in range(2):
        for core in range(2):
            start = zh * 32 + core * 16
            for a in range(4):
                out[zh * 8 + core * 4 + a] = total[start : start + 16, a * CUT : (a + 1) * CUT]


def last_body(got, out):
    for core in range(2):
        total = jnp.zeros((16, CUT), F32)
        for zh in range(2):
            for a in range(4):
                total = total + got[zh * 8 + core * 4 + a].astype(F32)
        out[:, core * CUT : (core + 1) * CUT] = total


def unpack_body(p0, p1, p2, p3, weight_out, pooled_out, mean_out, bias_out):
    at = home()
    for m, piece in enumerate((p0, p1, p2, p3)):
        columns = pl.ds(pl.multiple_of((at[0] ^ m) * CUT, CUT), CUT)
        weight_out[:, columns] = piece[0:BLOCK, :].astype(F32)
        extra = piece[BLOCK : BLOCK + EXTRA, :].astype(F32)
        pooled_out[:, columns] = extra[0:8] + extra[8:16]
        mean_out[:, columns] = extra[16:17] + extra[17:18]
        bias_out[:, columns] = extra[18:19] + extra[19:20]


def here(value):
    return pltpu.with_memory_space_constraint(value, pltpu.HBM)


def pack(lengths, hidden, rep_cotangent):
    return pl.pallas_call(
        packet_body,
        out_shape=pltpu.VMEM((8, PACK, LANES), BF16),
        in_specs=[SMEM(), pl.BlockSpec(memory_space=pltpu.HBM), pl.BlockSpec(memory_space=pltpu.HBM)],
        out_specs=VMEM(),
        scratch_shapes=[
            pltpu.VMEM((128, LANES), BF16),
            pltpu.VMEM((128, LANES), BF16),
            pltpu.VMEM((8, 1024), F32),
            pltpu.SemaphoreType.DMA((3,)),
        ],
        compiler_params=pltpu.CompilerParams(vmem_limit_bytes=8 << 20),
        name="packet",
    )(here(lengths), here(hidden), here(rep_cotangent))


def cut(head_weight):
    return pl.pallas_call(
        weights_body,
        out_shape=[pltpu.VMEM((BLOCK, CUT), BF16)] * 4,
        in_specs=[pl.BlockSpec(memory_space=pltpu.HBM)],
        out_specs=[VMEM()] * 4,
        scratch_shapes=[pltpu.SemaphoreType.DMA((4,))],
        compiler_params=pltpu.CompilerParams(vmem_limit_bytes=8 << 20),
        name="weights",
    )(here(head_weight))


def shape(dims, kind=BF16):
    return jax.ShapeDtypeStruct(dims, kind)


def per_device(hidden, head_weight, head_bias, rep_cotangent, lengths):
    def swap(value, axis, size, m):
        return lax.ppermute(value, axis, [(i, i ^ m) for i in range(size)])

    def trade(value, axes):
        return lax.all_to_all(value, axes, 0, 0, tiled=True)

    w = cut(head_weight)
    w = [w[0]] + [swap(w[m], "zq", 4, m) for m in (1, 2, 3)]

    packets = pack(lengths, hidden, rep_cotangent)
    got = trade(packets, ("zp", "zq"))
    rows, cot, lens = call(
        compact_body,
        [shape((16, HALF, LANES)), shape((SEQS, CUT), F32), shape((SEQS, LANES), F32)],
        [got],
        name="compact",
    )
    own = trade(rows, ("y", "x"))
    other = swap(own, "c", 2, 1)
    seg, segt, spread = call(
        tables_body,
        [shape((SEQS, LIVE)), shape((LIVE, LANES)), shape((TOKENS, LIVE))],
        [lens],
        flops=10_000_000,
        moved=2_000_000,
        name="tables",
    )
    mine, all_rows = call(
        logits_body,
        [shape((LIVE, CUT)), shape((4, LIVE, BLOCK))],
        [own, other, *w],
        2 * LIVE * 2048 * CUT,
        4 << 20,
        name="logits",
    )
    theirs = swap(mine, "zp", 2, 1)
    halves = call(halves_body, shape((4, CUT, CUT)), w, 0, 1 << 20, name="halves")
    halves = swap(halves, "c", 2, 1)
    grad, *extra = call(
        grads_body,
        [shape((LIVE, CUT))] + [shape((EXTRA, CUT))] * 4,
        [mine, theirs, head_bias.reshape(4, CUT), cot, seg, segt],
        name="grads",
    )
    partner = swap(grad, "c", 2, 1)
    pieces = call(
        weight_grad_body,
        [shape((BLOCK + EXTRA, CUT))] * 4,
        [all_rows, grad, *extra],
        2 * LIVE * 2048 * CUT,
        4 << 20,
        name="weight_grad",
    )
    pieces = [pieces[0]] + [swap(pieces[m], "zq", 4, m) for m in (1, 2, 3)]
    product = call(
        input_body,
        shape((TOKENS, 1024)),
        [spread, grad, partner, *w, halves],
        2 * TOKENS * 1024 * BLOCK,
        4 << 20,
        name="input",
    )
    plane = trade(product.reshape(16, 64, 1024), ("y", "x"))
    column = call(plane_body, shape((16, 16, CUT)), [plane], name="plane")
    column = trade(column, ("zh", "c", "zq"))
    input_grad = call(last_body, shape((16, BLOCK), F32), [column], name="last")
    weight_grad, pooled, mean, bias_grad = call(
        unpack_body,
        [shape((BLOCK, 1024), F32), shape((8, 1024), F32), shape((1, 1024), F32), shape((1, 1024), F32)],
        [*pieces],
        name="unpack",
    )
    return pooled, mean.reshape(1024), bias_grad.reshape(1024), weight_grad, input_grad


def solution(mesh):
    fine = Mesh(mesh.devices.reshape(2, 4, 2, 2, 4, 4), ("zh", "y", "c", "zp", "zq", "x"))
    dp = ("zp", "zq")
    columns = ("zh", "y", "c", "x")

    return jax.shard_map(
        per_device,
        mesh=fine,
        in_specs=(P(dp, None), P(dp, columns), P(columns), P(dp, columns), P(dp)),
        out_specs=(P(dp, columns), P(columns), P(columns), P(dp, columns), P(columns, dp)),
        check_vma=False,
    )
```

```python
import functools

import jax
import jax.numpy as jnp
from jax import lax
from jax.experimental import pallas as pl
from jax.experimental.pallas import tpu as pltpu
from jax.sharding import Mesh
from jax.sharding import PartitionSpec as P


F32 = jnp.float32
BF16 = jnp.bfloat16
I32 = jnp.int32

SEQS = 64
LEN = 16
TOKENS = SEQS * LEN
LIVE = SEQS * LEN * 5 // 8
HALF = LIVE // 2
QUART = LIVE // 4
LANES = 128
CUT = 256
BLOCK = 512
PACK = 96
EXTRA = 32

VMEM = functools.partial(pl.BlockSpec, memory_space=pltpu.VMEM)
SMEM = functools.partial(pl.BlockSpec, memory_space=pltpu.SMEM)


def call(body, outs, ins, flops=0, moved=0, name=None):
    return kernel(body, outs, ins, flops, moved, name)


def kernel(body, outs, ins, flops, moved, name):
    if name not in FREE:
        ins = [pltpu.with_memory_space_constraint(x, pltpu.VMEM) for x in ins]
    place = pltpu.VMEM if name in KEEP else pltpu.HBM if name in LEAVE else None
    return pl.pallas_call(
        body,
        out_shape=jax.tree.map(lambda o: place(o.shape, o.dtype), outs) if place else outs,
        in_specs=[VMEM()] * len(ins),
        out_specs=jax.tree.map(lambda _: VMEM(), outs),
        compiler_params=pltpu.CompilerParams(vmem_limit_bytes=20 << 20),
        cost_estimate=pl.CostEstimate(flops=flops, bytes_accessed=moved, transcendentals=0),
    )(*ins)


KEEP = ("compact", "grads", "halves", "plane", "tables")
LEAVE = ("input",)
FREE = ("weight_grad", "unpack")


def home():
    return lax.axis_index("zq"), lax.axis_index("zp"), lax.axis_index("c")


def iota(shape, dim):
    return lax.broadcasted_iota(I32, shape, dim)


def split(value):
    high = value.astype(BF16)
    return high, (value - high.astype(F32)).astype(BF16)


def dot(left, right, dims=((1,), (0,))):
    return lax.dot_general(left, right, (dims, ((), ())), preferred_element_type=F32)


def weights_body(w_ref, o0, o1, o2, o3, sems):
    at = home()
    copies = []
    for m, out in enumerate((o0, o1, o2, o3)):
        start = pl.multiple_of((at[0] ^ m) * CUT, CUT)
        copies.append(pltpu.make_async_copy(w_ref.at[:, pl.ds(start, CUT)], out, sems.at[m]))
        copies[-1].start()
    for copy in copies:
        copy.wait()


def packet_body(lengths, hidden_ref, cot_hbm, out, near_ref, far_ref, cot_ref, sems):
    spot = (4 * lax.axis_index("y") + lax.axis_index("x")) * LANES
    copies = []
    for i, ref in enumerate((near_ref, far_ref)):
        start = pl.multiple_of(spot + i * 2048, LANES)
        copies.append(pltpu.make_async_copy(hidden_ref.at[:, pl.ds(start, LANES)], ref, sems.at[i]))
    copies.append(pltpu.make_async_copy(cot_hbm, cot_ref, sems.at[2]))
    for copy in copies:
        copy.start()
    for copy in copies:
        copy.wait()
    row = iota((16, LANES), 0)
    lens = jnp.zeros((16, LANES), F32)
    for s in range(8):
        lens = jnp.where(row == s, lengths[s].astype(F32), lens)
    lens = lens.astype(BF16)
    first = iota((64, LANES), 1) < 64
    low_core = lax.axis_index("c") == 0
    folded = []
    for ref in (near_ref, far_ref):
        top, bottom = ref[0:64, :].astype(F32), ref[64:128, :].astype(F32)
        zero = jnp.where(first, top, pltpu.roll(bottom, 64, 1))
        one = jnp.where(first, pltpu.roll(top, 64, 1), bottom)
        folded.append(jnp.where(low_core, zero, one).astype(BF16))
    for a in range(4):
        part = cot_ref[:, a * CUT : (a + 1) * CUT]
        part = jnp.concatenate([part[:, :LANES], part[:, LANES:]], axis=0).astype(BF16)
        for q in range(2):
            k = 4 * q + a
            out[k, 0:64, :] = folded[q]
            out[k, 64:80, :] = lens
            out[k, 80:96, :] = part


def compact_body(got, out_a, out_b, cot_out, len_out):
    column = jnp.concatenate([got[k, 64:80, :].astype(F32)[0:8] for k in range(8)], axis=0)
    len_out[...] = column
    wide = jnp.broadcast_to(column[:, 0:1], (SEQS, TOKENS // 2))
    seq = iota((SEQS, TOKENS // 2), 0)
    index = iota((SEQS, TOKENS // 2), 1)
    tokens = jnp.concatenate([got[k, 0:64, :] for k in range(8)], axis=0)
    rows = iota((LIVE, TOKENS // 2), 0)
    chosen = []
    for half in range(2):
        owner = (index // 64) * 8 + half * 4 + (index % 64) // LEN
        start = jnp.sum(jnp.where(seq < owner, wide, 0.0), axis=0, keepdims=True)
        length = jnp.sum(jnp.where(seq == owner, wide, 0.0), axis=0, keepdims=True)
        place = iota((1, TOKENS // 2), 1) % LEN
        spot = jnp.where(place.astype(F32) < length, start.astype(I32) + place, -1)
        pick = jnp.where(jnp.broadcast_to(spot, rows.shape) == rows, 1.0, 0.0).astype(BF16)
        chosen.append(dot(pick, tokens))
    first = iota((QUART, LANES), 1) < 64
    for part, out in enumerate((out_a, out_b)):
        start, middle, end = part * HALF, part * HALF + QUART, part * HALF + HALF
        early = chosen[0][start:middle] + pltpu.roll(chosen[1][start:middle], 64, 1)
        late = pltpu.roll(chosen[0][middle:end], 64, 1) + chosen[1][middle:end]
        folded = jnp.where(first, early, late).astype(BF16)
        for j in range(16):
            out[j] = folded
    for k in range(8):
        cot = got[k, 80:96, :].astype(F32)
        cot_out[k * 8 : (k + 1) * 8, 0:LANES] = cot[0:8]
        cot_out[k * 8 : (k + 1) * 8, LANES:CUT] = cot[8:16]


def tables_body(len_ref, seg_ref, segt_ref, spread_ref):
    lens = len_ref[...]
    sub = iota((SEQS, LANES), 0)
    lane = iota((SEQS, LANES), 1)
    start_row = jnp.sum(jnp.where(sub < lane, lens, 0.0), axis=0, keepdims=True)
    len_row = jnp.sum(jnp.where(sub == lane, lens, 0.0), axis=0, keepdims=True)
    start_col = jnp.sum(
        jnp.where(lane < sub, jnp.broadcast_to(len_row, (SEQS, LANES)), 0.0), axis=1, keepdims=True
    )
    spot = iota((SEQS, LIVE), 1).astype(F32)
    first = jnp.broadcast_to(start_col, (SEQS, LIVE))
    last = jnp.broadcast_to(start_col + lens[:, 0:1], (SEQS, LIVE))
    seg_ref[...] = jnp.where((spot >= first) & (spot < last), 1.0, 0.0).astype(BF16)
    spot = iota((LIVE, LANES), 0).astype(F32)
    first = jnp.broadcast_to(start_row, (LIVE, LANES))
    last = jnp.broadcast_to(start_row + len_row, (LIVE, LANES))
    inside = (spot >= first) & (spot < last) & (iota((LIVE, LANES), 1) < SEQS)
    segt_ref[...] = jnp.where(inside, 1.0, 0.0).astype(BF16)
    row = iota((TOKENS, LANES), 0)
    lane = iota((TOKENS, LANES), 1)
    which = ((((row >> 5) & 1) * 4 + (row >> 8)) * 2 + ((row >> 4) & 1)) * 4 + ((row >> 6) & 3)
    per_row = jnp.broadcast_to(len_row, (TOKENS, LANES))
    start = jnp.sum(jnp.where(lane < which, per_row, 0.0), axis=1, keepdims=True)
    length = jnp.sum(jnp.where(lane == which, per_row, 0.0), axis=1, keepdims=True)
    place = (row[:, 0:1] & 15).astype(F32)
    spot = jnp.where(place < length, start + place, -1.0)
    target = iota((TOKENS, LIVE), 1).astype(F32)
    spread_ref[...] = jnp.where(jnp.broadcast_to(spot, (TOKENS, LIVE)) == target, 1.0, 0.0).astype(BF16)


def logits_body(own, other, w0, w1, w2, w3, out, rows_out):
    at = home()

    def unfold(low, high):
        first = iota((QUART, LANES), 1) < 64
        for j in range(16):
            left, right = low[j], high[j]
            columns = pl.ds((j % 4) * LANES, LANES)
            rows_out[j // 4, 0:QUART, columns] = jnp.where(first, left, pltpu.roll(right, 64, 1))
            rows_out[j // 4, QUART:HALF, columns] = jnp.where(first, pltpu.roll(left, 64, 1), right)

    @pl.when(at[2] == 0)
    def _():
        unfold(own, other)

    @pl.when(at[2] == 1)
    def _():
        unfold(other, own)

    total = jnp.zeros((HALF, CUT), F32)
    for m, w in enumerate((w0, w1, w2, w3)):
        total = total + dot(rows_out[at[0] ^ m], w[...])
    out[...] = total.astype(BF16)


def grads_body(mine_a, mine_b, theirs_a, theirs_b, bias, cot, seg, segt, grad_out, x0, x1, x2, x3):
    at = home()
    logits = jnp.concatenate(
        [
            mine_a[...].astype(F32) + theirs_a[...].astype(F32),
            mine_b[...].astype(F32) + theirs_b[...].astype(F32),
        ],
        axis=0,
    )
    logits = logits + bias[pl.ds(at[0], 1), :]
    positive = jnp.maximum(logits, 0.0)
    act = jnp.log1p(positive)
    cube = act * act * act
    high, low = split(cube * act)
    total = 1.0 + (dot(seg[...], high) + dot(seg[...], low))
    second = jnp.sqrt(total)
    fourth = jnp.sqrt(second)
    pooled = fourth - 1.0
    mean = jnp.sum(pooled, axis=0, keepdims=True) / SEQS
    pull = (cot[...] + mean) / (second * fourth)
    pad = jnp.zeros((LANES - SEQS, CUT), BF16)
    high, low = split(pull)
    spread = dot(segt[...], jnp.concatenate([high, pad], axis=0))
    spread = spread + dot(segt[...], jnp.concatenate([low, pad], axis=0))
    grad = spread * (cube / (1.0 + positive))
    bias_grad = jnp.sum(grad, axis=0, keepdims=True)
    grad_out[...] = grad.astype(BF16)
    m_high, m_low = split(mean)
    b_high, b_low = split(bias_grad)
    row = iota((16, CUT), 0)
    tail = jnp.zeros((16, CUT), F32)
    for i, v in enumerate((m_high, m_low, b_high, b_low)):
        tail = jnp.where(row == i, jnp.broadcast_to(v.astype(F32), (16, CUT)), tail)
    tail = tail.astype(BF16)
    for m, out in enumerate((x0, x1, x2, x3)):
        k = at[1] * 4 + (at[0] ^ m)
        mine8 = jnp.zeros((8, CUT), F32)
        for i in range(8):
            mine8 = jnp.where(k == i, pooled[i * 8 : (i + 1) * 8], mine8)
        high, low = split(mine8)
        out[0:16, :] = jnp.concatenate([high.astype(F32), low.astype(F32)], axis=0).astype(BF16)
        out[16:32, :] = tail


def weight_grad_body(rows_a, rows_b, grad, x0, x1, x2, x3, o0, o1, o2, o3):
    at = home()
    for m, (extra, out) in enumerate(zip((x0, x1, x2, x3), (o0, o1, o2, o3))):
        total = dot(rows_a[at[0] ^ m], grad[0:HALF, :], ((0,), (0,)))
        total = total + dot(rows_b[at[0] ^ m], grad[HALF:LIVE, :], ((0,), (0,)))
        out[0:BLOCK, :] = total.astype(BF16)
        out[BLOCK : BLOCK + EXTRA, :] = extra[...]


def halves_body(w0, w1, w2, w3, out):
    start = pl.multiple_of((1 - lax.axis_index("c")) * CUT, CUT)
    for m, w in enumerate((w0, w1, w2, w3)):
        out[m] = w[pl.ds(start, CUT), :]


def input_body(spread, grad, partner, w0, w1, w2, w3, half, out):
    at = home()
    start = pl.multiple_of(at[2] * CUT, CUT)
    mine = dot(spread[...], grad[...]).astype(BF16)
    theirs = dot(spread[...], partner[...]).astype(BF16)
    for m, w in enumerate((w0, w1, w2, w3)):
        total = dot(mine, w[pl.ds(start, CUT), :], ((1,), (1,)))
        total = total + dot(theirs, half[m], ((1,), (1,)))
        out[:, pl.ds(pl.multiple_of((at[0] ^ m) * CUT, CUT), CUT)] = total.astype(BF16)


def plane_body(got, out):
    total = got[0].astype(F32)
    for i in range(1, 16):
        total = total + got[i].astype(F32)
    total = total.astype(BF16)
    for zh in range(2):
        for core in range(2):
            start = zh * 32 + core * 16
            for a in range(4):
                out[zh * 8 + core * 4 + a] = total[start : start + 16, a * CUT : (a + 1) * CUT]


def last_body(got, out):
    for core in range(2):
        total = jnp.zeros((16, CUT), F32)
        for zh in range(2):
            for a in range(4):
                total = total + got[zh * 8 + core * 4 + a].astype(F32)
        out[:, core * CUT : (core + 1) * CUT] = total


def unpack_body(p0, p1, p2, p3, weight_out, pooled_out, mean_out, bias_out):
    at = home()
    for m, piece in enumerate((p0, p1, p2, p3)):
        columns = pl.ds(pl.multiple_of((at[0] ^ m) * CUT, CUT), CUT)
        weight_out[:, columns] = piece[0:BLOCK, :].astype(F32)
        extra = piece[BLOCK : BLOCK + EXTRA, :].astype(F32)
        pooled_out[:, columns] = extra[0:8] + extra[8:16]
        mean_out[:, columns] = extra[16:17] + extra[17:18]
        bias_out[:, columns] = extra[18:19] + extra[19:20]


def here(value):
    return pltpu.with_memory_space_constraint(value, pltpu.HBM)


def pack(lengths, hidden, rep_cotangent):
    return pl.pallas_call(
        packet_body,
        out_shape=pltpu.VMEM((8, PACK, LANES), BF16),
        in_specs=[SMEM(), pl.BlockSpec(memory_space=pltpu.HBM), pl.BlockSpec(memory_space=pltpu.HBM)],
        out_specs=VMEM(),
        scratch_shapes=[
            pltpu.VMEM((128, LANES), BF16),
            pltpu.VMEM((128, LANES), BF16),
            pltpu.VMEM((8, 1024), F32),
            pltpu.SemaphoreType.DMA((3,)),
        ],
        compiler_params=pltpu.CompilerParams(vmem_limit_bytes=8 << 20),
        name="packet",
    )(here(lengths), here(hidden), here(rep_cotangent))


def cut(head_weight):
    return pl.pallas_call(
        weights_body,
        out_shape=[pltpu.VMEM((BLOCK, CUT), BF16)] * 4,
        in_specs=[pl.BlockSpec(memory_space=pltpu.HBM)],
        out_specs=[VMEM()] * 4,
        scratch_shapes=[pltpu.SemaphoreType.DMA((4,))],
        compiler_params=pltpu.CompilerParams(vmem_limit_bytes=8 << 20),
        name="weights",
    )(here(head_weight))


def shape(dims, kind=BF16):
    return jax.ShapeDtypeStruct(dims, kind)


def per_device(hidden, head_weight, head_bias, rep_cotangent, lengths):
    def swap(value, axis, size, m):
        return lax.ppermute(value, axis, [(i, i ^ m) for i in range(size)])

    def trade(value, axes):
        return lax.all_to_all(value, axes, 0, 0, tiled=True)

    w = cut(head_weight)
    w = [w[0]] + [swap(w[m], "zq", 4, m) for m in (1, 2, 3)]

    packets = pack(lengths, hidden, rep_cotangent)
    got = trade(packets, ("zp", "zq"))
    rows_a, rows_b, cot, lens = call(
        compact_body,
        [shape((16, QUART, LANES))] * 2 + [shape((SEQS, CUT), F32), shape((SEQS, LANES), F32)],
        [got],
        name="compact",
    )
    seg, segt, spread = call(
        tables_body,
        [shape((SEQS, LIVE)), shape((LIVE, LANES)), shape((TOKENS, LIVE))],
        [lens],
        flops=10_000_000,
        moved=2_000_000,
        name="tables",
    )
    mine, theirs, kept = [], [], []
    for part, rows in (("a", rows_a), ("b", rows_b)):
        own = trade(rows, ("y", "x"))
        other = swap(own, "c", 2, 1)
        logits, whole_rows = call(
            logits_body,
            [shape((HALF, CUT)), pltpu.HBM((4, HALF, BLOCK), BF16)],
            [own, other, *w],
            2 * HALF * 2048 * CUT,
            3 << 20,
            name=f"logits_{part}",
        )
        mine.append(logits)
        kept.append(whole_rows)
        theirs.append(swap(logits, "zp", 2, 1))
    halves = call(halves_body, shape((4, CUT, CUT)), w, 0, 1 << 20, name="halves")
    halves = swap(halves, "c", 2, 1)
    grad, *extra = call(
        grads_body,
        [shape((LIVE, CUT))] + [shape((EXTRA, CUT))] * 4,
        [*mine, *theirs, head_bias.reshape(4, CUT), cot, seg, segt],
        name="grads",
    )
    partner = swap(grad, "c", 2, 1)
    pieces = call(
        weight_grad_body,
        [shape((BLOCK + EXTRA, CUT))] * 4,
        [*kept, grad, *extra],
        2 * LIVE * 2048 * CUT,
        4 << 20,
        name="weight_grad",
    )
    pieces = [pieces[0]] + [swap(pieces[m], "zq", 4, m) for m in (1, 2, 3)]
    product = call(
        input_body,
        shape((TOKENS, 1024)),
        [spread, grad, partner, *w, halves],
        2 * TOKENS * 1024 * BLOCK,
        4 << 20,
        name="input",
    )
    plane = trade(product.reshape(16, 64, 1024), ("y", "x"))
    column = call(plane_body, shape((16, 16, CUT)), [plane], name="plane")
    column = trade(column, ("zh", "c", "zq"))
    input_grad = call(last_body, shape((16, BLOCK), F32), [column], name="last")
    weight_grad, pooled, mean, bias_grad = call(
        unpack_body,
        [shape((BLOCK, 1024), F32), shape((8, 1024), F32), shape((1, 1024), F32), shape((1, 1024), F32)],
        [*pieces],
        name="unpack",
    )
    return pooled, mean.reshape(1024), bias_grad.reshape(1024), weight_grad, input_grad


def solution(mesh):
    fine = Mesh(mesh.devices.reshape(2, 4, 2, 2, 4, 4), ("zh", "y", "c", "zp", "zq", "x"))
    dp = ("zp", "zq")
    columns = ("zh", "y", "c", "x")

    return jax.shard_map(
        per_device,
        mesh=fine,
        in_specs=(P(dp, None), P(dp, columns), P(columns), P(dp, columns), P(dp)),
        out_specs=(P(dp, columns), P(columns), P(columns), P(dp, columns), P(columns, dp)),
        check_vma=False,
    )
```

```python
import functools

import jax
import jax.numpy as jnp
from jax import lax
from jax.experimental import pallas as pl
from jax.experimental.pallas import tpu as pltpu
from jax.sharding import Mesh
from jax.sharding import PartitionSpec as P


F32 = jnp.float32
BF16 = jnp.bfloat16
I32 = jnp.int32

SEQS = 64
LEN = 16
TOKENS = SEQS * LEN
LIVE = SEQS * LEN * 5 // 8
HALF = LIVE // 2
QUART = LIVE // 4
LANES = 128
CUT = 256
BLOCK = 512
PACK = 96
EXTRA = 32

VMEM = functools.partial(pl.BlockSpec, memory_space=pltpu.VMEM)
SMEM = functools.partial(pl.BlockSpec, memory_space=pltpu.SMEM)


def call(body, outs, ins, flops=0, moved=0, name=None):
    return kernel(body, outs, ins, flops, moved, name)


def kernel(body, outs, ins, flops, moved, name):
    if name not in FREE:
        ins = [pltpu.with_memory_space_constraint(x, pltpu.VMEM) for x in ins]
    place = pltpu.VMEM if name in KEEP else pltpu.HBM if name in LEAVE else None
    return pl.pallas_call(
        body,
        out_shape=jax.tree.map(lambda o: place(o.shape, o.dtype), outs) if place else outs,
        in_specs=[VMEM()] * len(ins),
        out_specs=jax.tree.map(lambda _: VMEM(), outs),
        compiler_params=pltpu.CompilerParams(vmem_limit_bytes=20 << 20),
        cost_estimate=pl.CostEstimate(flops=flops, bytes_accessed=moved, transcendentals=0),
    )(*ins)


KEEP = ("early", "compact", "grads", "halves", "plane", "tables")
LEAVE = ("input",)
FREE = ("weight_grad", "unpack")


def home():
    return lax.axis_index("zq"), lax.axis_index("zp"), lax.axis_index("c")


def iota(shape, dim):
    return lax.broadcasted_iota(I32, shape, dim)


def split(value):
    high = value.astype(BF16)
    return high, (value - high.astype(F32)).astype(BF16)


def dot(left, right, dims=((1,), (0,))):
    return lax.dot_general(left, right, (dims, ((), ())), preferred_element_type=F32)


def weights_body(w_ref, o0, o1, o2, o3, sems):
    at = home()
    copies = []
    for m, out in enumerate((o0, o1, o2, o3)):
        start = pl.multiple_of((at[0] ^ m) * CUT, CUT)
        copies.append(pltpu.make_async_copy(w_ref.at[:, pl.ds(start, CUT)], out, sems.at[m]))
        copies[-1].start()
    for copy in copies:
        copy.wait()


def packet_body(lengths, hidden_ref, cot_hbm, out, near_ref, far_ref, cot_ref, sems):
    spot = (4 * lax.axis_index("y") + lax.axis_index("x")) * LANES
    copies = []
    for i, ref in enumerate((near_ref, far_ref)):
        start = pl.multiple_of(spot + i * 2048, LANES)
        copies.append(pltpu.make_async_copy(hidden_ref.at[:, pl.ds(start, LANES)], ref, sems.at[i]))
    copies.append(pltpu.make_async_copy(cot_hbm, cot_ref, sems.at[2]))
    for copy in copies:
        copy.start()
    for copy in copies:
        copy.wait()
    row = iota((16, LANES), 0)
    lens = jnp.zeros((16, LANES), F32)
    for s in range(8):
        lens = jnp.where(row == s, lengths[s].astype(F32), lens)
    lens = lens.astype(BF16)
    first = iota((64, LANES), 1) < 64
    low_core = lax.axis_index("c") == 0
    folded = []
    for ref in (near_ref, far_ref):
        top, bottom = ref[0:64, :].astype(F32), ref[64:128, :].astype(F32)
        zero = jnp.where(first, top, pltpu.roll(bottom, 64, 1))
        one = jnp.where(first, pltpu.roll(top, 64, 1), bottom)
        folded.append(jnp.where(low_core, zero, one).astype(BF16))
    for a in range(4):
        part = cot_ref[:, a * CUT : (a + 1) * CUT]
        part = jnp.concatenate([part[:, :LANES], part[:, LANES:]], axis=0).astype(BF16)
        for q in range(2):
            k = 4 * q + a
            out[k, 0:64, :] = folded[q]
            out[k, 64:80, :] = lens
            out[k, 80:96, :] = part


def compact_body(got, out_a, out_b, cot_out, len_out):
    column = jnp.concatenate([got[k, 64:80, :].astype(F32)[0:8] for k in range(8)], axis=0)
    len_out[...] = column
    wide = jnp.broadcast_to(column[:, 0:1], (SEQS, TOKENS // 2))
    seq = iota((SEQS, TOKENS // 2), 0)
    index = iota((SEQS, TOKENS // 2), 1)
    tokens = jnp.concatenate([got[k, 0:64, :] for k in range(8)], axis=0)
    rows = iota((LIVE, TOKENS // 2), 0)
    chosen = []
    for half in range(2):
        owner = (index // 64) * 8 + half * 4 + (index % 64) // LEN
        start = jnp.sum(jnp.where(seq < owner, wide, 0.0), axis=0, keepdims=True)
        length = jnp.sum(jnp.where(seq == owner, wide, 0.0), axis=0, keepdims=True)
        place = iota((1, TOKENS // 2), 1) % LEN
        spot = jnp.where(place.astype(F32) < length, start.astype(I32) + place, -1)
        pick = jnp.where(jnp.broadcast_to(spot, rows.shape) == rows, 1.0, 0.0).astype(BF16)
        chosen.append(dot(pick, tokens))
    first = iota((QUART, LANES), 1) < 64
    for part, out in enumerate((out_a, out_b)):
        start, middle, end = part * HALF, part * HALF + QUART, part * HALF + HALF
        early = chosen[0][start:middle] + pltpu.roll(chosen[1][start:middle], 64, 1)
        late = pltpu.roll(chosen[0][middle:end], 64, 1) + chosen[1][middle:end]
        folded = jnp.where(first, early, late).astype(BF16)
        for j in range(16):
            out[j] = folded
    for k in range(8):
        cot = got[k, 80:96, :].astype(F32)
        cot_out[k * 8 : (k + 1) * 8, 0:LANES] = cot[0:8]
        cot_out[k * 8 : (k + 1) * 8, LANES:CUT] = cot[8:16]


def tables_body(len_ref, seg_ref, segt_ref, spread_ref):
    lens = len_ref[...]
    sub = iota((SEQS, LANES), 0)
    lane = iota((SEQS, LANES), 1)
    start_row = jnp.sum(jnp.where(sub < lane, lens, 0.0), axis=0, keepdims=True)
    len_row = jnp.sum(jnp.where(sub == lane, lens, 0.0), axis=0, keepdims=True)
    start_col = jnp.sum(
        jnp.where(lane < sub, jnp.broadcast_to(len_row, (SEQS, LANES)), 0.0), axis=1, keepdims=True
    )
    spot = iota((SEQS, LIVE), 1).astype(F32)
    first = jnp.broadcast_to(start_col, (SEQS, LIVE))
    last = jnp.broadcast_to(start_col + lens[:, 0:1], (SEQS, LIVE))
    seg_ref[...] = jnp.where((spot >= first) & (spot < last), 1.0, 0.0).astype(BF16)
    spot = iota((LIVE, LANES), 0).astype(F32)
    first = jnp.broadcast_to(start_row, (LIVE, LANES))
    last = jnp.broadcast_to(start_row + len_row, (LIVE, LANES))
    inside = (spot >= first) & (spot < last) & (iota((LIVE, LANES), 1) < SEQS)
    segt_ref[...] = jnp.where(inside, 1.0, 0.0).astype(BF16)
    row = iota((TOKENS, LANES), 0)
    lane = iota((TOKENS, LANES), 1)
    which = ((((row >> 5) & 1) * 4 + (row >> 8)) * 2 + ((row >> 4) & 1)) * 4 + ((row >> 6) & 3)
    per_row = jnp.broadcast_to(len_row, (TOKENS, LANES))
    start = jnp.sum(jnp.where(lane < which, per_row, 0.0), axis=1, keepdims=True)
    length = jnp.sum(jnp.where(lane == which, per_row, 0.0), axis=1, keepdims=True)
    place = (row[:, 0:1] & 15).astype(F32)
    spot = jnp.where(place < length, start + place, -1.0)
    target = iota((TOKENS, LIVE), 1).astype(F32)
    spread_ref[...] = jnp.where(jnp.broadcast_to(spot, (TOKENS, LIVE)) == target, 1.0, 0.0).astype(BF16)


def logits_body(own, other, w0, w1, w2, w3, out, rows_out):
    at = home()

    def unfold(low, high):
        first = iota((QUART, LANES), 1) < 64
        for j in range(16):
            left, right = low[j], high[j]
            columns = pl.ds((j % 4) * LANES, LANES)
            rows_out[j // 4, 0:QUART, columns] = jnp.where(first, left, pltpu.roll(right, 64, 1))
            rows_out[j // 4, QUART:HALF, columns] = jnp.where(first, pltpu.roll(left, 64, 1), right)

    @pl.when(at[2] == 0)
    def _():
        unfold(own, other)

    @pl.when(at[2] == 1)
    def _():
        unfold(other, own)

    total = jnp.zeros((HALF, CUT), F32)
    for m, w in enumerate((w0, w1, w2, w3)):
        total = total + dot(rows_out[at[0] ^ m], w[...])
    out[...] = total.astype(BF16)


def activate(mine, theirs, bias, seg):
    logits = mine[...].astype(F32) + theirs[...].astype(F32) + bias[pl.ds(home()[0], 1), :]
    positive = jnp.maximum(logits, 0.0)
    act = jnp.log1p(positive)
    cube = act * act * act
    high, low = split(cube * act)
    return cube / (1.0 + positive), dot(seg, high) + dot(seg, low)


def early_body(mine, theirs, bias, seg, slope_out, sum_out):
    slope, total = activate(mine, theirs, bias, seg[...][:, 0:HALF])
    slope_out[...] = slope
    sum_out[...] = total


def grads_body(mine, theirs, slope_a, sum_a, bias, cot, seg, segt, grad_out, x0, x1, x2, x3):
    at = home()
    slope_b, sum_b = activate(mine, theirs, bias, seg[...][:, HALF:LIVE])
    total = 1.0 + (sum_a[...] + sum_b)
    second = jnp.sqrt(total)
    fourth = jnp.sqrt(second)
    pooled = fourth - 1.0
    mean = jnp.sum(pooled, axis=0, keepdims=True) / SEQS
    pull = (cot[...] + mean) / (second * fourth)
    pad = jnp.zeros((LANES - SEQS, CUT), BF16)
    high, low = split(pull)
    spread = dot(segt[...], jnp.concatenate([high, pad], axis=0))
    spread = spread + dot(segt[...], jnp.concatenate([low, pad], axis=0))
    grad = spread * jnp.concatenate([slope_a[...], slope_b], axis=0)
    bias_grad = jnp.sum(grad, axis=0, keepdims=True)
    grad_out[...] = grad.astype(BF16)
    m_high, m_low = split(mean)
    b_high, b_low = split(bias_grad)
    row = iota((16, CUT), 0)
    tail = jnp.zeros((16, CUT), F32)
    for i, v in enumerate((m_high, m_low, b_high, b_low)):
        tail = jnp.where(row == i, jnp.broadcast_to(v.astype(F32), (16, CUT)), tail)
    tail = tail.astype(BF16)
    for m, out in enumerate((x0, x1, x2, x3)):
        k = at[1] * 4 + (at[0] ^ m)
        mine8 = jnp.zeros((8, CUT), F32)
        for i in range(8):
            mine8 = jnp.where(k == i, pooled[i * 8 : (i + 1) * 8], mine8)
        high, low = split(mine8)
        out[0:16, :] = jnp.concatenate([high.astype(F32), low.astype(F32)], axis=0).astype(BF16)
        out[16:32, :] = tail


def weight_grad_body(rows_a, rows_b, grad, x0, x1, x2, x3, o0, o1, o2, o3):
    at = home()
    for m, (extra, out) in enumerate(zip((x0, x1, x2, x3), (o0, o1, o2, o3))):
        total = dot(rows_a[at[0] ^ m], grad[0:HALF, :], ((0,), (0,)))
        total = total + dot(rows_b[at[0] ^ m], grad[HALF:LIVE, :], ((0,), (0,)))
        out[0:BLOCK, :] = total.astype(BF16)
        out[BLOCK : BLOCK + EXTRA, :] = extra[...]


def halves_body(w0, w1, w2, w3, out):
    start = pl.multiple_of((1 - lax.axis_index("c")) * CUT, CUT)
    for m, w in enumerate((w0, w1, w2, w3)):
        out[m] = w[pl.ds(start, CUT), :]


def input_body(spread, grad, partner, w0, w1, w2, w3, half, out):
    at = home()
    start = pl.multiple_of(at[2] * CUT, CUT)
    mine = dot(spread[...], grad[...]).astype(BF16)
    theirs = dot(spread[...], partner[...]).astype(BF16)
    for m, w in enumerate((w0, w1, w2, w3)):
        total = dot(mine, w[pl.ds(start, CUT), :], ((1,), (1,)))
        total = total + dot(theirs, half[m], ((1,), (1,)))
        out[:, pl.ds(pl.multiple_of((at[0] ^ m) * CUT, CUT), CUT)] = total.astype(BF16)


def plane_body(got, out):
    total = got[0].astype(F32)
    for i in range(1, 16):
        total = total + got[i].astype(F32)
    total = total.astype(BF16)
    for zh in range(2):
        for core in range(2):
            start = zh * 32 + core * 16
            for a in range(4):
                out[zh * 8 + core * 4 + a] = total[start : start + 16, a * CUT : (a + 1) * CUT]


def last_body(got, out):
    for core in range(2):
        total = jnp.zeros((16, CUT), F32)
        for zh in range(2):
            for a in range(4):
                total = total + got[zh * 8 + core * 4 + a].astype(F32)
        out[:, core * CUT : (core + 1) * CUT] = total


def unpack_body(p0, p1, p2, p3, weight_out, pooled_out, mean_out, bias_out):
    at = home()
    for m, piece in enumerate((p0, p1, p2, p3)):
        columns = pl.ds(pl.multiple_of((at[0] ^ m) * CUT, CUT), CUT)
        weight_out[:, columns] = piece[0:BLOCK, :].astype(F32)
        extra = piece[BLOCK : BLOCK + EXTRA, :].astype(F32)
        pooled_out[:, columns] = extra[0:8] + extra[8:16]
        mean_out[:, columns] = extra[16:17] + extra[17:18]
        bias_out[:, columns] = extra[18:19] + extra[19:20]


def here(value):
    return pltpu.with_memory_space_constraint(value, pltpu.HBM)


def pack(lengths, hidden, rep_cotangent):
    return pl.pallas_call(
        packet_body,
        out_shape=pltpu.VMEM((8, PACK, LANES), BF16),
        in_specs=[SMEM(), pl.BlockSpec(memory_space=pltpu.HBM), pl.BlockSpec(memory_space=pltpu.HBM)],
        out_specs=VMEM(),
        scratch_shapes=[
            pltpu.VMEM((128, LANES), BF16),
            pltpu.VMEM((128, LANES), BF16),
            pltpu.VMEM((8, 1024), F32),
            pltpu.SemaphoreType.DMA((3,)),
        ],
        compiler_params=pltpu.CompilerParams(vmem_limit_bytes=8 << 20),
        name="packet",
    )(here(lengths), here(hidden), here(rep_cotangent))


def cut(head_weight):
    return pl.pallas_call(
        weights_body,
        out_shape=[pltpu.VMEM((BLOCK, CUT), BF16)] * 4,
        in_specs=[pl.BlockSpec(memory_space=pltpu.HBM)],
        out_specs=[VMEM()] * 4,
        scratch_shapes=[pltpu.SemaphoreType.DMA((4,))],
        compiler_params=pltpu.CompilerParams(vmem_limit_bytes=8 << 20),
        name="weights",
    )(here(head_weight))


def shape(dims, kind=BF16):
    return jax.ShapeDtypeStruct(dims, kind)


def per_device(hidden, head_weight, head_bias, rep_cotangent, lengths):
    def swap(value, axis, size, m):
        return lax.ppermute(value, axis, [(i, i ^ m) for i in range(size)])

    def trade(value, axes):
        return lax.all_to_all(value, axes, 0, 0, tiled=True)

    w = cut(head_weight)
    w = [w[0]] + [swap(w[m], "zq", 4, m) for m in (1, 2, 3)]

    packets = pack(lengths, hidden, rep_cotangent)
    got = trade(packets, ("zp", "zq"))
    rows_a, rows_b, cot, lens = call(
        compact_body,
        [shape((16, QUART, LANES))] * 2 + [shape((SEQS, CUT), F32), shape((SEQS, LANES), F32)],
        [got],
        name="compact",
    )
    seg, segt, spread = call(
        tables_body,
        [shape((SEQS, LIVE)), shape((LIVE, LANES)), shape((TOKENS, LIVE))],
        [lens],
        flops=10_000_000,
        moved=2_000_000,
        name="tables",
    )
    mine, theirs, kept = [], [], []
    for part, rows in (("a", rows_a), ("b", rows_b)):
        own = trade(rows, ("y", "x"))
        other = swap(own, "c", 2, 1)
        logits, whole_rows = call(
            logits_body,
            [shape((HALF, CUT)), pltpu.HBM((4, HALF, BLOCK), BF16)],
            [own, other, *w],
            2 * HALF * 2048 * CUT,
            3 << 20,
            name=f"logits_{part}",
        )
        mine.append(logits)
        kept.append(whole_rows)
        theirs.append(swap(logits, "zp", 2, 1))
    halves = call(halves_body, shape((4, CUT, CUT)), w, 0, 1 << 20, name="halves")
    halves = swap(halves, "c", 2, 1)
    bias = head_bias.reshape(4, CUT)
    early = call(
        early_body,
        [shape((HALF, CUT), F32), shape((SEQS, CUT), F32)],
        [mine[0], theirs[0], bias, seg],
        name="early",
    )
    grad, *extra = call(
        grads_body,
        [shape((LIVE, CUT))] + [shape((EXTRA, CUT))] * 4,
        [mine[1], theirs[1], *early, bias, cot, seg, segt],
        name="grads",
    )
    partner = swap(grad, "c", 2, 1)
    pieces = call(
        weight_grad_body,
        [shape((BLOCK + EXTRA, CUT))] * 4,
        [*kept, grad, *extra],
        2 * LIVE * 2048 * CUT,
        4 << 20,
        name="weight_grad",
    )
    pieces = [pieces[0]] + [swap(pieces[m], "zq", 4, m) for m in (1, 2, 3)]
    product = call(
        input_body,
        shape((TOKENS, 1024)),
        [spread, grad, partner, *w, halves],
        2 * TOKENS * 1024 * BLOCK,
        4 << 20,
        name="input",
    )
    plane = trade(product.reshape(16, 64, 1024), ("y", "x"))
    column = call(plane_body, shape((16, 16, CUT)), [plane], name="plane")
    column = trade(column, ("zh", "c", "zq"))
    input_grad = call(last_body, shape((16, BLOCK), F32), [column], name="last")
    weight_grad, pooled, mean, bias_grad = call(
        unpack_body,
        [shape((BLOCK, 1024), F32), shape((8, 1024), F32), shape((1, 1024), F32), shape((1, 1024), F32)],
        [*pieces],
        name="unpack",
    )
    return pooled, mean.reshape(1024), bias_grad.reshape(1024), weight_grad, input_grad


def solution(mesh):
    fine = Mesh(mesh.devices.reshape(2, 4, 2, 2, 4, 4), ("zh", "y", "c", "zp", "zq", "x"))
    dp = ("zp", "zq")
    columns = ("zh", "y", "c", "x")

    return jax.shard_map(
        per_device,
        mesh=fine,
        in_specs=(P(dp, None), P(dp, columns), P(columns), P(dp, columns), P(dp)),
        out_specs=(P(dp, columns), P(columns), P(columns), P(dp, columns), P(columns, dp)),
        check_vma=False,
    )
```
